32 devices in a mesh: blk: 8 (over y, x, core), grp: 4 (over z).
Axes of the slice: x: 2, y: 2, z: 4, core: 2. Of those that a mesh axis runs over, the one named last changes fastest.
Arguments:
- points: bfloat16 [16, 4096], P(None, ('blk', 'grp')), may hold values from -2 to 2, as said below
- right_side: float32 [64, 4096], P(None, ('blk', 'grp')), may hold values from -10 to 16
- nugget: float32 [4096], P(('blk', 'grp')), may hold values from 2 to 3
- scales: float32 [16], replicated, may hold values from 0.8 to 1.25
- pairs: int32 [8, 3], replicated, may hold values 0 or 1
Outputs:
- solution: float32 [64, 4096], P(None, ('blk', 'grp'))
- residual: float32 [64, 4096], P(None, ('blk', 'grp'))
The draws below stay inside these ranges and needn't reach their ends.
Inputs may be any that keep to these rules, and one draw needn't show every extreme that they name: pairs[b, d - 1] is 1 when block b and block (b + d) mod 8 share a tile. In features 0 and 1 the points of block b lie on the circle of radius 8 / (2 pi) about the anchor, at arc lengths from b to b + 3 + 1 (measured round the circle from feature 1 = 0), one point in each of 512 equal slots of that arc; features 2 to 15 lie between 0 and 0.3.
All inputs are finite; a program needn't handle non-finite values.
Results may differ from the reference program's by a relative error of at most 0.0006.
Values may be sent and summed in bfloat16 or wider, within the bound.
No kernel may reach another device: no remote copies, remote signals or barrier semaphores. Data moves between devices by JAX's collectives and lax.ppermute only.
A program may use at most 64 MiB of HBM per device.

```python
import math
import jax
import jax.numpy as jnp
from jax import lax

ROWS_DEV = 128
FEAT = 16
NRHS = 64
MAXP = 3
ITERS = 2
BLOCK = 512
NBLOCKS = 8
POINTS = 4096
N_BLK = 8
N_GRP = 4


def layout(key):
    slot_keys = jax.random.split(jax.random.fold_in(key, 1), NBLOCKS)
    places = jax.vmap(lambda each_key: jax.random.permutation(each_key, BLOCK))(slot_keys).astype(jnp.float32)
    jitter = jax.random.uniform(jax.random.fold_in(key, 2), (NBLOCKS, BLOCK), jnp.float32)
    anchor = jnp.arange(NBLOCKS, dtype=jnp.float32)[:, None]
    arc_pos = anchor + (MAXP + 1) * (places + jitter) / BLOCK
    angles = 2.0 * math.pi / NBLOCKS * arc_pos
    return angles.reshape(POINTS)


def draw_points(key, part):
    angles = layout(jax.random.fold_in(key, 11))
    radius = NBLOCKS / (2.0 * math.pi)
    circle = jnp.stack([radius * jnp.cos(angles), radius * jnp.sin(angles)], axis=0)
    other_key = jax.random.fold_in(key, 12)
    others = 0.2 * jax.random.uniform(other_key, (FEAT - 2, POINTS), jnp.float32)
    return jnp.concatenate([circle, others], axis=0).astype(jnp.bfloat16)


def draw_right_side(key, part):
    angles = layout(jax.random.fold_in(key, 11))
    level_key = jax.random.fold_in(key, 31)
    wave_key = jax.random.fold_in(key, 32)
    phase_key = jax.random.fold_in(key, 33)
    harmonic_key = jax.random.fold_in(key, 34)
    noise_key = jax.random.fold_in(key, 35)
    block_rank = jnp.repeat(jnp.arange(NBLOCKS, dtype=jnp.float32), BLOCK) / (NBLOCKS - 1)
    harmonic = jax.random.randint(harmonic_key, (NRHS, 1), 1, 4).astype(jnp.float32)
    phases = jax.random.uniform(phase_key, (NRHS, 1), jnp.float32, 0.0, 2.0 * math.pi)
    amplitude = jax.random.uniform(wave_key, (NRHS, 1), jnp.float32, 0.3, 0.8)
    wave_part = amplitude * jnp.cos(harmonic * angles[None, :] + phases)
    levels = jax.random.uniform(level_key, (NRHS, 1), jnp.float32, 0.6, 1.2)
    noise_part = 0.6 * jax.random.truncated_normal(noise_key, -4.0, 4.0, (NRHS, POINTS), jnp.float32)
    envelope = 1.0 + 2.0 * block_rank
    return (envelope[None, :] * (levels + wave_part + noise_part)).astype(jnp.float32)


def set_ends(entries, rng, least, top_value):
    index_at = [jax.random.randint(jax.random.fold_in(rng, axis), (), 0, length) for axis, length in enumerate(entries.shape)]
    widest = entries.shape.index(max(entries.shape))
    beside = index_at[:widest] + [(index_at[widest] + 1) % entries.shape[widest]] + index_at[widest + 1:]
    return entries.at[tuple(index_at)].set(least).at[tuple(beside)].set(top_value)


def shard_levels(own_key, extent, cuts, low, top_value):
    def one(axis_at, parts):
        draws = jax.random.uniform(jax.random.fold_in(jax.random.fold_in(own_key, 6), axis_at), (parts,), jnp.float32, low / len(cuts), top_value / len(cuts))
        return jnp.repeat(jnp.exp(draws), extent[axis_at] // parts).reshape((-1,) + (1,) * (len(extent) - axis_at - 1))

    level = one(*cuts[0])
    for cut in cuts[1:]:
        level = level * one(*cut)
    return level


def setup_inputs(seed: int = 0) -> dict:
    streams_of = jax.random.split(jax.random.key(seed), 6)
    points = draw_points(jax.random.fold_in(streams_of[5], 71), 0)
    right_side = draw_right_side(jax.random.fold_in(streams_of[5], 71), 0)
    nugget = jnp.clip(jnp.exp(math.log(3.0) - 0.4054651 * jax.random.uniform(streams_of[2], (POINTS,), jnp.float32) ** shard_levels(streams_of[2], (POINTS,), ((0, 32),), -0.2, 0.2)), 2.0, 3.0)
    scales = jnp.clip(jnp.exp(jax.random.uniform(streams_of[3], (FEAT,), jnp.float32, math.log(0.8), math.log(1.25))), 0.8, 1.25)
    pairs = set_ends((jax.random.randint(streams_of[4], (NBLOCKS, MAXP), 0, 3) < 2).astype(jnp.int32), jax.random.fold_in(streams_of[4], 1), 0, 1)
    return {"points": points, "right_side": right_side, "nugget": nugget, "scales": scales, "pairs": pairs}


def kernel_tile(row_z, col_z):
    cross = jnp.dot(row_z.T, col_z, precision=lax.Precision.HIGHEST, preferred_element_type=jnp.float32)
    squared = lax.optimization_barrier(jnp.sum(row_z * row_z, axis=0))[:, None] + lax.optimization_barrier(jnp.sum(col_z * col_z, axis=0))[None, :] - 2.0 * cross
    distance = jnp.sqrt(jnp.maximum(squared, 0.0))
    spare = jnp.maximum(1.0 - distance, 0.0)
    return (spare ** 4 * (4.0 * distance + 1.0)).astype(jnp.bfloat16)

def reference(points, right_side, nugget, scales, pairs):
    block = ROWS_DEV * N_GRP
    nblocks = N_BLK
    amp = 1.0 / (block + 16)
    scaled = points.astype(jnp.float32) / scales[:, None]

    def operate(direction):
        rounded = direction.astype(jnp.bfloat16).astype(jnp.float32)

        def visit(acc, index):
            start = (index * block).astype(jnp.int32)
            row_z = lax.dynamic_slice_in_dim(scaled, start, block, 1)
            row_v = lax.dynamic_slice_in_dim(rounded, start, block, 1)
            for offset in range(MAXP + 1):
                other = ((index + offset) % nblocks * block).astype(jnp.int32)
                col_z = lax.dynamic_slice_in_dim(scaled, other, block, 1)
                col_v = lax.dynamic_slice_in_dim(rounded, other, block, 1)
                tile = kernel_tile(row_z, col_z).astype(jnp.float32)
                if offset == 0:
                    weight = jnp.float32(1.0)
                else:
                    weight = pairs[index, offset - 1].astype(jnp.float32)
                ahead = weight * jnp.dot(col_v, tile.T, preferred_element_type=jnp.float32)
                current = lax.dynamic_slice_in_dim(acc, start, block, 1)
                acc = lax.dynamic_update_slice_in_dim(acc, current + ahead, start, 1)
                if offset > 0:
                    behind = weight * jnp.dot(row_v, tile, preferred_element_type=jnp.float32)
                    current = lax.dynamic_slice_in_dim(acc, other, block, 1)
                    acc = lax.dynamic_update_slice_in_dim(acc, current + behind, other, 1)
            return (acc, None)
        empty = jnp.zeros(direction.shape, jnp.float32)
        acc, unused = lax.scan(visit, empty, jnp.arange(nblocks, dtype=jnp.int32))
        return nugget[None, :] * direction + amp * acc
    solution = jnp.zeros(right_side.shape, jnp.float32)
    residual = right_side
    direction = right_side
    norm_now = lax.optimization_barrier(jnp.sum(residual * residual, axis=1))
    for step in range(ITERS):
        image = operate(direction)
        alpha = norm_now / lax.optimization_barrier(jnp.sum(direction * image, axis=1))
        solution = solution + alpha[:, None] * direction
        residual = residual - alpha[:, None] * image
        if step + 1 < ITERS:
            norm_next = lax.optimization_barrier(jnp.sum(residual * residual, axis=1))
            direction = residual + (norm_next / norm_now)[:, None] * direction
            norm_now = norm_next
    return (solution, residual)
```

```python
import functools

import jax
import jax.numpy as jnp
from jax import lax
from jax.experimental import pallas as pl
from jax.experimental.pallas import tpu as pltpu
from jax.sharding import PartitionSpec as P

THETA = 2.5
BF16 = jnp.bfloat16
F32 = jnp.float32
VMEM = pl.BlockSpec(memory_space=pltpu.VMEM)
SMEM = pl.BlockSpec(memory_space=pltpu.SMEM)


def chip_hops(nblk, maxp):
    pairs = nblk // 2
    reach = (maxp + 1) // 2
    if pairs <= 2 * reach + 1 and pairs & (pairs - 1) == 0:
        hops = [k for k in range(1, pairs)]
        there = lambda i, k: 2 * ((i // 2) ^ k) + i % 2
    else:
        hops = sorted({s % pairs for s in range(-reach, reach + 1)} - {0})
        there = lambda i, k: (i + 2 * k) % nblk
    return hops, there


def split3(value):
    high = value.astype(BF16)
    rest = value - high.astype(F32)
    middle = rest.astype(BF16)
    low = (rest - middle.astype(F32)).astype(BF16)
    return high, middle, low


def norm_rows(norm, first, ones_first):
    at = lax.broadcasted_iota(jnp.int32, (16, norm.shape[1]), 0)
    high, middle, low = (part.astype(F32) for part in split3(norm))
    rows = jnp.where((at >= ones_first) & (at < ones_first + 3), 1.0, 0.0)
    rows = jnp.where(at == first, high, rows)
    rows = jnp.where(at == first + 1, middle, rows)
    rows = jnp.where(at == first + 2, low, rows)
    return rows.astype(BF16)


def weight_of(pairs_ref, here, other, nblk, maxp):
    ahead = lax.rem(other - here + nblk, nblk)
    back = nblk - ahead
    in_ahead = (ahead >= 1) & (ahead <= maxp)
    in_back = (back >= 1) & (back <= maxp)
    first = pairs_ref[here, jnp.clip(ahead - 1, 0, maxp - 1)]
    second = pairs_ref[other, jnp.clip(back - 1, 0, maxp - 1)]
    return jnp.where(ahead == 0, 1, jnp.where(in_ahead, first, 0) + jnp.where(in_back, second, 0))


def slot_block(here, slot, hops, nblk):
    pairs = nblk // 2
    hop = ([0] + hops)[slot // 2]
    chip = here // 2
    if hops == list(range(1, pairs)) and pairs & (pairs - 1) == 0:
        chip = chip ^ hop
    else:
        chip = lax.rem(chip + hop, pairs)
    return 2 * chip + (lax.rem(here, 2) ^ (slot % 2))


def first_kernel(hops, ngrp, maxp, nblk, amp, pairs_ref, here_ref, scales_ref, nugget_ref, side_ref, *refs):
    nhop = len(hops)
    row_refs, refs = refs[:ngrp], refs[ngrp:]
    pair_refs, refs = refs[: nhop + 2], refs[nhop + 2 :]
    k_ref, own_ref, message_refs, (row_f, acc) = refs[0], refs[1], refs[2 : 1 + ngrp], refs[1 + ngrp :]
    feat, rows = row_refs[0].shape
    nrhs = side_ref.shape[0]
    here = here_ref[0]
    scales = scales_ref[...]
    weigh = -2.0 / (scales * scales)
    parts = []
    for ref in row_refs:
        point = ref[...].astype(F32)
        norm = jnp.sum((point / scales) ** 2, axis=0, keepdims=True)
        point = ref[...]
        parts.append(jnp.concatenate([point, point, point, norm_rows(norm, 0, 3)], axis=0))
    for at, part in enumerate(parts):
        row_f[pl.ds(at * rows, rows), :] = part.astype(F32).T.astype(BF16)
    acc[...] = jnp.zeros_like(acc)
    for slot in range(2 * (nhop + 1)):
        other = slot_block(here, slot, hops, nblk)
        weight = weight_of(pairs_ref, here, other, nblk, maxp)
        if slot < 2:
            stacked_ref, base = pair_refs[slot], 0
        else:
            stacked_ref, base = pair_refs[1 + slot // 2], (slot % 2) * (feat + nrhs)

        @pl.when(weight != 0)
        def visit(slot=slot, stacked_ref=stacked_ref, base=base, weight=weight):
            point = stacked_ref[pl.ds(base, feat), :].astype(F32)
            vector = stacked_ref[pl.ds(base + feat, nrhs), :]
            norm = jnp.sum((point / scales) ** 2, axis=0, keepdims=True)
            col_f = jnp.concatenate([*split3(point * weigh), norm_rows(norm, 3, 0)], axis=0)
            for at in range(ngrp):
                squared = jnp.maximum(
                    jnp.dot(row_f[pl.ds(at * rows, rows), :], col_f, preferred_element_type=F32), 1e-30
                )
                spare = jnp.maximum(1.0 - squared * lax.rsqrt(squared), 0.0)
                square = spare * spare
                tile = (square * square * (5.0 - 4.0 * spare)).astype(BF16)
                k_ref[pl.ds(at * rows, rows), pl.ds(slot * rows, rows)] = tile
                acc[:, pl.ds(at * rows, rows)] += weight.astype(F32) * lax.dot_general(
                    vector, tile, (((1,), (1,)), ((), ())), preferred_element_type=F32
                )

    own_ref[...] = amp * acc[...]
    own_ref[:, :rows] += (nugget_ref[...] - THETA) * side_ref[...]
    high = own_ref[...].astype(BF16)
    for at, ref in enumerate(message_refs, 1):
        part = pl.ds(at * rows, rows)
        ref[:, : rows * ngrp] = high
        ref[:, rows * ngrp :] = (own_ref[:, part] - own_ref[:, part].astype(BF16).astype(F32)).astype(BF16)


def second_kernel(hops, ngrp, maxp, nblk, pairs_ref, here_ref, own_ref, k_ref, *refs):
    nhop = len(hops)
    message_refs, (w_ref, same_ref, cross_ref, rounded) = refs[: ngrp - 1], refs[ngrp - 1 :]
    nrhs, rows = w_ref.shape
    here = here_ref[0]
    for at in range(ngrp):
        part = pl.ds(at * rows, rows)
        total = own_ref[:, part]
        for step, ref in enumerate(message_refs, 1):
            total += ref[:, pl.ds((at ^ step) * rows, rows)].astype(F32)
            if at == 0:
                total += ref[:, rows * ngrp :].astype(F32)
        if at == 0:
            w_ref[...] = total
        rounded[:, part] = total.astype(BF16)
    for slot in range(2 * (nhop + 1)):
        other = slot_block(here, slot, hops, nblk)
        weight = weight_of(pairs_ref, here, other, nblk, maxp)
        to_ref = (same_ref, cross_ref)[slot % 2]
        part = pl.ds(slot // 2 * rows, rows)

        @pl.when(weight != 0)
        def visit(slot=slot, to_ref=to_ref, part=part, weight=weight):
            to_ref[:, part] = weight.astype(F32) * jnp.dot(
                rounded[...], k_ref[:, pl.ds(slot * rows, rows)], preferred_element_type=F32
            )

        @pl.when(weight == 0)
        def skip(to_ref=to_ref, part=part):
            to_ref[:, part] = jnp.zeros((nrhs, rows), F32)


def third_kernel(amp, nugget_ref, side_ref, w_ref, part_ref, *refs):
    sums, (u_ref, dots_ref) = refs[:-2], refs[-2:]
    nrhs = side_ref.shape[0]
    total = part_ref[...]
    for ref in sums:
        total += ref[...]
    b, w = side_ref[...], w_ref[...]
    u = nugget_ref[...] * w + amp * total
    u_ref[...] = u
    columns = [jnp.sum(x * y, axis=1, keepdims=True) for x, y in ((b, b), (b, w), (w, w), (b, u), (w, u))]
    at = lax.broadcasted_iota(jnp.int32, (nrhs, 128), 1)
    table = jnp.zeros((nrhs, 128), F32)
    for place, column in enumerate(columns):
        table = jnp.where(at == place, column, table)
    table = table.T[:8]
    for device in range(dots_ref.shape[0]):
        dots_ref[device] = table


def last_kernel(side_ref, w_ref, u_ref, dots_ref, solution_ref, residual_ref):
    nrhs = side_ref.shape[0]
    rows = jnp.sum(dots_ref[...], axis=0)
    table = jnp.concatenate([rows, jnp.zeros((120, nrhs), F32)], axis=0).T
    bb, bw, ww, bu, wu = (table[:, at : at + 1] for at in range(5))
    b, w, u = side_ref[...], w_ref[...], u_ref[...]
    b_image = bw + THETA * bb
    alpha = bb / b_image
    keep = 1.0 - alpha * THETA
    norm = keep * keep * bb - 2.0 * keep * alpha * bw + alpha * alpha * ww
    c = keep + norm / bb
    curve = c * c * b_image - c * alpha * (bu + ww + THETA * bw) + alpha * alpha * wu
    step = norm / curve
    direction = c * b - alpha * w
    solution_ref[...] = alpha * b + step * direction
    residual_ref[...] = keep * b - alpha * w - step * (c * w + (c * THETA) * b - alpha * u)


def on_device(points, right_side, nugget, scales, pairs):
    nblk = lax.axis_size("blk")
    ngrp = lax.axis_size("grp")
    feat, rows = points.shape
    nrhs = right_side.shape[0]
    maxp = pairs.shape[1]
    total = rows * ngrp
    amp = 1.0 / (total + 16)
    hops, there = chip_hops(nblk, maxp)
    slots = 2 * (len(hops) + 1)
    here = lax.axis_index("blk").astype(jnp.int32).reshape(1)
    nugget = nugget[None, :]

    def from_core(value):
        return lax.ppermute(value, "blk", [(i ^ 1, i) for i in range(nblk)])

    def from_chip(value, hop):
        return lax.ppermute(value, "blk", [(there(i, hop), i) for i in range(nblk)])

    def to_chip(value, hop):
        return lax.ppermute(value, "blk", [(i, there(i, hop)) for i in range(nblk)])

    def across(value, step):
        return lax.ppermute(value, "grp", [(i ^ step, i) for i in range(ngrp)])

    stacked = jnp.concatenate([points, right_side.astype(BF16)], axis=0)
    beside = from_core(stacked)
    pair = jnp.concatenate([stacked, beside], axis=0)
    partners = [from_chip(pair, hop) for hop in hops]
    row_points = [points] + [across(points, step) for step in range(1, ngrp)]

    k_tiles, own, *messages = pl.pallas_call(
        functools.partial(first_kernel, hops, ngrp, maxp, nblk, amp),
        out_shape=[
            jax.ShapeDtypeStruct((total, slots * rows), BF16),
            jax.ShapeDtypeStruct((nrhs, total), F32),
        ]
        + [jax.ShapeDtypeStruct((nrhs, total + rows), BF16)] * (ngrp - 1),
        in_specs=[SMEM, SMEM] + [VMEM] * (3 + ngrp + 2 + len(hops)),
        out_specs=[VMEM] * (1 + ngrp),
        scratch_shapes=[pltpu.VMEM((total, 64), BF16), pltpu.VMEM((nrhs, total), F32)],
        name="tiles",
    )(pairs, here, scales[:, None], nugget, right_side, *row_points, stacked, beside, *partners)

    messages = [across(message, step) for step, message in enumerate(messages, 1)]
    w, same, cross = pl.pallas_call(
        functools.partial(second_kernel, hops, ngrp, maxp, nblk),
        out_shape=[
            jax.ShapeDtypeStruct((nrhs, rows), F32),
            jax.ShapeDtypeStruct((nrhs, slots // 2 * rows), F32),
            jax.ShapeDtypeStruct((nrhs, slots // 2 * rows), F32),
        ],
        in_specs=[SMEM, SMEM] + [VMEM] * (1 + ngrp),
        out_specs=[VMEM] * 3,
        scratch_shapes=[pltpu.VMEM((nrhs, total), BF16)],
        name="back",
    )(pairs, here, own, k_tiles, *messages)

    summed = same + from_core(cross)
    pieces = [summed[:, at * rows : (at + 1) * rows] for at in range(slots // 2)]
    pieces = [pieces[0]] + [to_chip(piece, hop) for piece, hop in zip(pieces[1:], hops)]
    u, dots = pl.pallas_call(
        functools.partial(third_kernel, amp),
        out_shape=[
            jax.ShapeDtypeStruct((nrhs, rows), F32),
            jax.ShapeDtypeStruct((nblk * ngrp, 8, nrhs), F32),
        ],
        in_specs=[VMEM] * (3 + len(pieces)),
        out_specs=[VMEM] * 2,
        name="dots",
    )(nugget, right_side, w, *pieces)
    dots = lax.all_to_all(dots, ("blk", "grp"), 0, 0)
    return pl.pallas_call(
        last_kernel,
        out_shape=[jax.ShapeDtypeStruct((nrhs, rows), F32)] * 2,
        in_specs=[VMEM] * 4,
        out_specs=[VMEM] * 2,
        name="outputs",
    )(right_side, w, u, dots)


def solution(mesh):
    placed = (P(None, ("blk", "grp")), P(None, ("blk", "grp")), P(("blk", "grp")), P(), P())
    return jax.shard_map(
        on_device,
        mesh=mesh,
        in_specs=placed,
        out_specs=(P(None, ("blk", "grp")), P(None, ("blk", "grp"))),
        check_vma=False,
    )
```

```python
import functools

import jax
import jax.numpy as jnp
from jax import lax
from jax.experimental import pallas as pl
from jax.experimental.pallas import tpu as pltpu
from jax.sharding import PartitionSpec as P

THETA = 2.5
BF16 = jnp.bfloat16
F32 = jnp.float32
VMEM = pl.BlockSpec(memory_space=pltpu.VMEM)
SMEM = pl.BlockSpec(memory_space=pltpu.SMEM)
PARAMS = pltpu.CompilerParams(vmem_limit_bytes=24 << 20)


def chip_hops(nblk, maxp):
    pairs = nblk // 2
    reach = (maxp + 1) // 2
    if pairs <= 2 * reach + 1 and pairs & (pairs - 1) == 0:
        hops = [k for k in range(1, pairs)]
        there = lambda i, k: 2 * ((i // 2) ^ k) + i % 2
    else:
        hops = sorted({s % pairs for s in range(-reach, reach + 1)} - {0})
        there = lambda i, k: (i + 2 * k) % nblk
    return hops, there


def split3(value):
    high = value.astype(BF16)
    rest = value - high.astype(F32)
    middle = rest.astype(BF16)
    low = (rest - middle.astype(F32)).astype(BF16)
    return high, middle, low


def norm_rows(norm, first, ones_first):
    at = lax.broadcasted_iota(jnp.int32, (16, norm.shape[1]), 0)
    high, middle, low = (part.astype(F32) for part in split3(norm))
    rows = jnp.where((at >= ones_first) & (at < ones_first + 3), 1.0, 0.0)
    rows = jnp.where(at == first, high, rows)
    rows = jnp.where(at == first + 1, middle, rows)
    rows = jnp.where(at == first + 2, low, rows)
    return rows.astype(BF16)


def weight_of(pairs_ref, here, other, nblk, maxp):
    ahead = lax.rem(other - here + nblk, nblk)
    back = nblk - ahead
    in_ahead = (ahead >= 1) & (ahead <= maxp)
    in_back = (back >= 1) & (back <= maxp)
    first = pairs_ref[jnp.clip(ahead - 1, 0, maxp - 1), here]
    second = pairs_ref[jnp.clip(back - 1, 0, maxp - 1), other]
    return jnp.where(ahead == 0, 1, jnp.where(in_ahead, first, 0) + jnp.where(in_back, second, 0))


def slot_block(here, slot, hops, nblk):
    pairs = nblk // 2
    hop = ([0] + hops)[slot // 2]
    chip = here // 2
    if hops == list(range(1, pairs)) and pairs & (pairs - 1) == 0:
        chip = chip ^ hop
    else:
        chip = lax.rem(chip + hop, pairs)
    return 2 * chip + (lax.rem(here, 2) ^ (slot % 2))


def first_kernel(hops, ngrp, maxp, nblk, amp, pairs_ref, scales_ref, nugget_ref, side_ref, *refs):
    nhop = len(hops)
    row_refs, refs = refs[:ngrp], refs[ngrp:]
    pair_refs, refs = refs[: nhop + 2], refs[nhop + 2 :]
    k_ref, own_ref, message_refs, (row_f, acc) = refs[0], refs[1], refs[2 : 1 + ngrp], refs[1 + ngrp :]
    feat, rows = row_refs[0].shape
    nrhs = side_ref.shape[0]
    here = lax.axis_index("blk")
    eye = lax.broadcasted_iota(jnp.int32, (feat, feat), 0) == lax.broadcasted_iota(jnp.int32, (feat, feat), 1)
    scales = jnp.sum(jnp.where(eye, scales_ref[...], 0.0), axis=1, keepdims=True)
    weigh = -2.0 / (scales * scales)
    parts = []
    for ref in row_refs:
        point = ref[...].astype(F32)
        norm = jnp.sum((point / scales) ** 2, axis=0, keepdims=True)
        point = ref[...]
        parts.append(jnp.concatenate([point, point, point, norm_rows(norm, 0, 3)], axis=0))
    for at, part in enumerate(parts):
        row_f[pl.ds(at * rows, rows), :] = part.astype(F32).T.astype(BF16)
    acc[...] = jnp.zeros_like(acc)
    for slot in range(2 * (nhop + 1)):
        other = slot_block(here, slot, hops, nblk)
        weight = weight_of(pairs_ref, here, other, nblk, maxp)
        if slot < 2:
            stacked_ref, base = pair_refs[slot], 0
        else:
            stacked_ref, base = pair_refs[1 + slot // 2], (slot % 2) * (feat + nrhs)

        @pl.when(weight != 0)
        def visit(slot=slot, stacked_ref=stacked_ref, base=base, weight=weight):
            point = stacked_ref[pl.ds(base, feat), :].astype(F32)
            vector = stacked_ref[pl.ds(base + feat, nrhs), :]
            norm = jnp.sum((point / scales) ** 2, axis=0, keepdims=True)
            col_f = jnp.concatenate([*split3(point * weigh), norm_rows(norm, 3, 0)], axis=0)
            for at in range(ngrp):
                squared = jnp.maximum(
                    jnp.dot(row_f[pl.ds(at * rows, rows), :], col_f, preferred_element_type=F32), 1e-30
                )
                spare = jnp.maximum(1.0 - squared * lax.rsqrt(squared), 0.0)
                square = spare * spare
                tile = (square * square * (5.0 - 4.0 * spare)).astype(BF16)
                k_ref[pl.ds(at * rows, rows), pl.ds(slot * rows, rows)] = tile
                acc[:, pl.ds(at * rows, rows)] += weight.astype(F32) * lax.dot_general(
                    vector, tile, (((1,), (1,)), ((), ())), preferred_element_type=F32
                )

    own_ref[...] = amp * acc[...]
    own_ref[:, :rows] += (nugget_ref[...] - THETA) * side_ref[...]
    high = own_ref[...].astype(BF16)
    for at, ref in enumerate(message_refs, 1):
        part = pl.ds(at * rows, rows)
        ref[:, : rows * ngrp] = high
        ref[:, rows * ngrp :] = (own_ref[:, part] - own_ref[:, part].astype(BF16).astype(F32)).astype(BF16)


def second_kernel(hops, ngrp, maxp, nblk, pairs_ref, own_ref, k_ref, *refs):
    nhop = len(hops)
    message_refs, (w_ref, cross_ref, *same_refs, rounded) = refs[: ngrp - 1], refs[ngrp - 1 :]
    nrhs, rows = w_ref.shape
    here = lax.axis_index("blk")
    for at in range(ngrp):
        part = pl.ds(at * rows, rows)
        total = own_ref[:, part]
        for step, ref in enumerate(message_refs, 1):
            total += ref[:, pl.ds((at ^ step) * rows, rows)].astype(F32)
            if at == 0:
                total += ref[:, rows * ngrp :].astype(F32)
        if at == 0:
            w_ref[...] = total
        rounded[:, part] = total.astype(BF16)
    for slot in range(2 * (nhop + 1)):
        other = slot_block(here, slot, hops, nblk)
        weight = weight_of(pairs_ref, here, other, nblk, maxp)
        to_ref, part = (cross_ref, pl.ds(slot // 2 * rows, rows)) if slot % 2 else (same_refs[slot // 2], pl.ds(0, rows))

        @pl.when(weight != 0)
        def visit(slot=slot, to_ref=to_ref, part=part, weight=weight):
            to_ref[:, part] = weight.astype(F32) * jnp.dot(
                rounded[...], k_ref[:, pl.ds(slot * rows, rows)], preferred_element_type=F32
            )

        @pl.when(weight == 0)
        def skip(to_ref=to_ref, part=part):
            to_ref[:, part] = jnp.zeros((nrhs, rows), F32)


def columns_of(nrhs, *pairs):
    at = lax.broadcasted_iota(jnp.int32, (nrhs, 128), 1)
    table = jnp.zeros((nrhs, 128), F32)
    for place, (x, y) in enumerate(pairs):
        table = jnp.where(at == place, jnp.sum(x * y, axis=1, keepdims=True), table)
    return table


def third_kernel(amp, nugget_ref, side_ref, w_ref, part_ref, *refs):
    sums, (u_ref, dots_ref) = refs[:-2], refs[-2:]
    nrhs = side_ref.shape[0]
    total = part_ref[...]
    for ref in sums:
        total += ref[...]
    b, w = side_ref[...], w_ref[...]
    u = nugget_ref[...] * w + amp * total
    u_ref[...] = u
    upper = columns_of(nrhs, (b, b), (w, w), (w, u))
    lower = columns_of(nrhs, (b, w), (b, u))
    table = jnp.concatenate([upper, lower], axis=0).T
    for place in range(3):
        row = table[place : place + 1]
        part = pl.ds(2 * nrhs * place, 2 * nrhs)
        dots_ref[:, :, part] = jnp.broadcast_to(row[None], (dots_ref.shape[0], 1, 2 * nrhs))


def last_kernel(side_ref, w_ref, u_ref, dots_ref, solution_ref, residual_ref):
    nrhs = side_ref.shape[0]
    row = jnp.sum(dots_ref[...], axis=0)
    width = 2 * nrhs
    at = lax.broadcasted_iota(jnp.int32, (8, width), 0)
    table = jnp.zeros((8, width), F32)
    for place in range(3):
        table = jnp.where(at == place, row[:, place * width : (place + 1) * width], table)
    table = jnp.concatenate([table, jnp.zeros((120, width), F32)], axis=0).T
    bb, ww, wu = (table[:nrhs, at : at + 1] for at in range(3))
    bw, bu = (table[nrhs : 2 * nrhs, at : at + 1] for at in range(2))
    b, w, u = side_ref[...], w_ref[...], u_ref[...]
    b_image = bw + THETA * bb
    alpha = bb / b_image
    keep = 1.0 - alpha * THETA
    norm = keep * keep * bb - 2.0 * keep * alpha * bw + alpha * alpha * ww
    c = keep + norm / bb
    curve = c * c * b_image - c * alpha * (bu + ww + THETA * bw) + alpha * alpha * wu
    step = norm / curve
    direction = c * b - alpha * w
    solution_ref[...] = alpha * b + step * direction
    residual_ref[...] = keep * b - alpha * w - step * (c * w + (c * THETA) * b - alpha * u)


def on_device(points, right_side, nugget, scales, pairs):
    nblk = lax.axis_size("blk")
    ngrp = lax.axis_size("grp")
    feat, rows = points.shape
    nrhs = right_side.shape[0]
    maxp = pairs.shape[1]
    total = rows * ngrp
    amp = 1.0 / (total + 16)
    hops, there = chip_hops(nblk, maxp)
    slots = 2 * (len(hops) + 1)
    nugget = nugget[None, :]

    def from_core(value):
        return lax.ppermute(value, "blk", [(i ^ 1, i) for i in range(nblk)])

    def from_chip(value, hop):
        return lax.ppermute(value, "blk", [(there(i, hop), i) for i in range(nblk)])

    def to_chip(value, hop):
        return lax.ppermute(value, "blk", [(i, there(i, hop)) for i in range(nblk)])

    def across(value, step):
        return lax.ppermute(value, "grp", [(i ^ step, i) for i in range(ngrp)])

    stacked = jnp.concatenate([points, right_side.astype(BF16)], axis=0)
    beside = from_core(stacked)
    pair = jnp.concatenate([stacked, beside], axis=0)
    partners = [from_chip(pair, hop) for hop in hops]
    row_points = [points] + [across(points, step) for step in range(1, ngrp)]

    k_tiles, own, *messages = pl.pallas_call(
        functools.partial(first_kernel, hops, ngrp, maxp, nblk, amp),
        out_shape=[
            jax.ShapeDtypeStruct((total, slots * rows), BF16),
            jax.ShapeDtypeStruct((nrhs, total), F32),
        ]
        + [jax.ShapeDtypeStruct((nrhs, total + rows), BF16)] * (ngrp - 1),
        in_specs=[SMEM] + [VMEM] * (3 + ngrp + 2 + len(hops)),
        out_specs=[VMEM] * (1 + ngrp),
        scratch_shapes=[pltpu.VMEM((total, 64), BF16), pltpu.VMEM((nrhs, total), F32)],
        compiler_params=PARAMS,
        name="tiles",
    )(pairs.T, scales[None, :], nugget, right_side, *row_points, stacked, beside, *partners)

    messages = [across(message, step) for step, message in enumerate(messages, 1)]
    w, cross, *same = pl.pallas_call(
        functools.partial(second_kernel, hops, ngrp, maxp, nblk),
        out_shape=[
            jax.ShapeDtypeStruct((nrhs, rows), F32),
            jax.ShapeDtypeStruct((nrhs, slots // 2 * rows), F32),
        ]
        + [jax.ShapeDtypeStruct((nrhs, rows), F32)] * (slots // 2),
        in_specs=[SMEM] + [VMEM] * (1 + ngrp),
        out_specs=[VMEM] * (2 + slots // 2),
        scratch_shapes=[pltpu.VMEM((nrhs, total), BF16)],
        compiler_params=PARAMS,
        name="back",
    )(pairs.T, own, k_tiles, *messages)

    cross = from_core(cross)
    pieces = [part + cross[:, at * rows : (at + 1) * rows] for at, part in enumerate(same)]
    pieces = [pieces[0]] + [to_chip(piece, hop) for piece, hop in zip(pieces[1:], hops)]
    u, dots = pl.pallas_call(
        functools.partial(third_kernel, amp),
        out_shape=[
            jax.ShapeDtypeStruct((nrhs, rows), F32),
            jax.ShapeDtypeStruct((nblk * ngrp, 1, 6 * nrhs), F32),
        ],
        in_specs=[VMEM] * (3 + len(pieces)),
        out_specs=[VMEM] * 2,
        compiler_params=PARAMS,
        name="dots",
    )(nugget, right_side, w, *pieces)
    dots = lax.all_to_all(dots, ("blk", "grp"), 0, 0)
    return pl.pallas_call(
        last_kernel,
        out_shape=[jax.ShapeDtypeStruct((nrhs, rows), F32)] * 2,
        in_specs=[VMEM] * 4,
        out_specs=[VMEM] * 2,
        compiler_params=PARAMS,
        name="outputs",
    )(right_side, w, u, dots)


def solution(mesh):
    placed = (P(None, ("blk", "grp")), P(None, ("blk", "grp")), P(("blk", "grp")), P(), P())
    return jax.shard_map(
        on_device,
        mesh=mesh,
        in_specs=placed,
        out_specs=(P(None, ("blk", "grp")), P(None, ("blk", "grp"))),
        check_vma=False,
    )
```

```python
import functools

import jax
import jax.numpy as jnp
from jax import lax
from jax.experimental import pallas as pl
from jax.experimental.pallas import tpu as pltpu
from jax.sharding import PartitionSpec as P

THETA = 2.5
REACH = 4.0
BF16 = jnp.bfloat16
F32 = jnp.float32
VMEM = pl.BlockSpec(memory_space=pltpu.VMEM)
PARAMS = pltpu.CompilerParams(vmem_limit_bytes=24 << 20)


def power_of_two(n):
    return n & (n - 1) == 0


class Plane:
    def __init__(self, nblk, maxp):
        self.nblk, self.maxp = nblk, maxp
        self.chips = nblk // 2
        reach = (maxp + 1) // 2
        self.doubling = self.chips <= 2 * reach + 1 and power_of_two(self.chips)
        if self.doubling:
            self.hops = list(range(self.chips))
        else:
            self.hops = [0] + sorted({s % self.chips for s in range(-reach, reach + 1)} - {0})
        self.slots = 2 * len(self.hops)
        self.live = [slot for slot in range(self.slots) if any(self.near(b, slot) for b in range(nblk))]

    def block(self, here, slot):
        chip = here // 2
        hop = self.hops[slot // 2]
        chip = chip ^ hop if self.doubling else (chip + hop) % self.chips
        return 2 * chip + ((here % 2) ^ (slot % 2))

    def near(self, here, slot):
        ahead = (self.block(here, slot) - here) % self.nblk
        return min(ahead, self.nblk - ahead) <= self.maxp

    def there(self, here, hop):
        return 2 * (here // 2 ^ hop if self.doubling else (here // 2 + hop) % self.chips) + here % 2


def split3(value):
    high = value.astype(BF16)
    rest = value - high.astype(F32)
    middle = rest.astype(BF16)
    low = (rest - middle.astype(F32)).astype(BF16)
    return high, middle, low


def norm_rows(norm, first, ones_first):
    at = lax.broadcasted_iota(jnp.int32, (16, norm.shape[1]), 0)
    high, middle, low = (part.astype(F32) for part in split3(norm))
    rows = jnp.where((at >= ones_first) & (at < ones_first + 3), 1.0, 0.0)
    rows = jnp.where(at == first, high, rows)
    rows = jnp.where(at == first + 1, middle, rows)
    rows = jnp.where(at == first + 2, low, rows)
    return rows.astype(BF16)


def column_of(row):
    size = row.shape[1]
    eye = lax.broadcasted_iota(jnp.int32, (size, size), 0) == lax.broadcasted_iota(jnp.int32, (size, size), 1)
    return jnp.sum(jnp.where(eye, row, 0.0), axis=1, keepdims=True)


def weight_of(plane, pairs, here, slot):
    nblk, maxp = plane.nblk, plane.maxp
    chip = here // 2
    hop = plane.hops[slot // 2]
    chip = chip ^ hop if plane.doubling else lax.rem(chip + hop, plane.chips)
    other = 2 * chip + (lax.rem(here, 2) ^ (slot % 2))
    ahead = lax.rem(other - here + nblk, nblk)
    offset = lax.broadcasted_iota(jnp.int32, pairs.shape, 0) + 1
    block = lax.broadcasted_iota(jnp.int32, pairs.shape, 1)
    taken = ((block == here) & (offset == ahead)).astype(F32) + ((block == other) & (offset == nblk - ahead)).astype(F32)
    return jnp.sum(jnp.sum(taken * pairs, axis=0, keepdims=True), axis=1, keepdims=True)


def tile_columns(slots, at_slot, base, stacked, scales, row_f, weights_ref, k_ref):
    feat = scales.shape[0]
    rows = stacked[0].shape[1]
    weigh = -2.0 * (REACH / scales) * (REACH / scales)
    vectors = []
    for place, slot in enumerate(slots):
        block = stacked[at_slot[slot]]
        point = block[:feat].astype(F32)
        norm = jnp.sum((point * (REACH / scales)) ** 2, axis=0, keepdims=True)
        col_f = jnp.concatenate([*split3(point * weigh), norm_rows(norm, 3, 0)], axis=0)
        weight = weights_ref[:, pl.ds(slot * rows, rows)].astype(BF16)
        vectors.append(block[feat:] * weight)
        for at in range(row_f.shape[0] // rows):
            part = pl.ds(at * rows, rows)
            squared = jnp.maximum(jnp.dot(row_f[part, :], col_f, preferred_element_type=F32), 1e-30)
            spare = jnp.maximum(REACH - squared * lax.rsqrt(squared), 0.0)
            square = spare * spare
            k_ref[part, pl.ds((base + place) * rows, rows)] = (square * square * (5.0 - spare)).astype(BF16)
    return jnp.concatenate(vectors, axis=1)


def near_kernel(plane, slots, pairs_ref, scales_ref, near_ref, far_ref, stacked_ref, row_f, weights_ref, k_ref, acc_ref):
    feat = scales_ref.shape[1]
    rows = near_ref.shape[1]
    here = lax.axis_index("blk")
    pairs = pairs_ref[...].astype(F32)
    for slot in range(plane.slots):
        weight = jnp.ones((1, 1), F32) if slot == 0 else weight_of(plane, pairs, here, slot)
        weights_ref[:, pl.ds(slot * rows, rows)] = jnp.broadcast_to(weight, (1, rows))
    scales = column_of(scales_ref[...])
    place = 0
    for ref in (near_ref, far_ref):
        for at in range(ref.shape[0] // feat):
            block = ref[pl.ds(at * feat, feat), :]
            norm = jnp.sum((block.astype(F32) * (REACH / scales)) ** 2, axis=0, keepdims=True)
            part = jnp.concatenate([block, block, block, norm_rows(norm, 0, 3)], axis=0)
            row_f[pl.ds(place * rows, rows), :] = part.astype(F32).T.astype(BF16)
            place += 1
    height = stacked_ref.shape[0] // len(slots)
    stacked = [stacked_ref[pl.ds(at * height, height), :] for at in range(len(slots))]
    vector = tile_columns(slots, {slot: at for at, slot in enumerate(slots)}, 0, stacked, scales, row_f, weights_ref, k_ref)
    acc_ref[...] = lax.dot_general(vector, k_ref[...], (((1,), (1,)), ((), ())), preferred_element_type=F32)


def far_kernel(slots, at_slot, amp, scales_ref, nugget_ref, side_ref, row_f, weights_ref, acc_ref, *refs):
    nstack = len(refs) - 2 - (row_f.shape[0] // side_ref.shape[1] - 1)
    stacked_refs, (k_ref, own_ref, *message_refs) = refs[:nstack], refs[nstack:]
    nrhs, rows = side_ref.shape
    height = scales_ref.shape[1] + nrhs
    total = row_f.shape[0]
    stacked = [ref[pl.ds(at, height), :] for ref in stacked_refs for at in range(0, ref.shape[0], height)]
    scales = column_of(scales_ref[...])
    vector = tile_columns(slots, at_slot, 0, stacked, scales, row_f, weights_ref, k_ref)
    whole = acc_ref[...] + lax.dot_general(
        vector, k_ref[...], (((1,), (1,)), ((), ())), preferred_element_type=F32
    )
    own_ref[...] = amp * whole
    own_ref[:, :rows] += (nugget_ref[...] - THETA) * side_ref[...]
    high = own_ref[...].astype(BF16)
    for at, ref in enumerate(message_refs, 1):
        part = pl.ds(at * rows, rows)
        ref[:, :total] = high
        ref[:, total:] = (own_ref[:, part] - own_ref[:, part].astype(BF16).astype(F32)).astype(BF16)


def cross_kernel(near, far, weights_ref, own_ref, near_ref, far_ref, *refs):
    outs = 2 + count_cross(near, far)
    message_refs, (w_ref, rounded_ref, *cross_refs) = refs[:-outs], refs[-outs:]
    rows = w_ref.shape[1]
    for at in range(own_ref.shape[1] // rows):
        part = pl.ds(at * rows, rows)
        total = own_ref[:, part]
        for step, ref in enumerate(message_refs, 1):
            total += ref[:, pl.ds((at ^ step) * rows, rows)].astype(F32)
            if at == 0:
                total += ref[:, own_ref.shape[1] :].astype(F32)
        if at == 0:
            w_ref[...] = total
        rounded_ref[:, part] = total.astype(BF16)
    contribute(near, far, 1, weights_ref, rounded_ref, near_ref, far_ref, cross_refs)


def count_cross(near, far):
    return sum(slot % 2 for slot in near + far)


def contribute(near, far, side, weights_ref, rounded_ref, near_ref, far_ref, out_refs):
    rows = near_ref.shape[1] // len(near)
    out = 0
    for slots, k_ref in ((near, near_ref), (far, far_ref)):
        for place, slot in enumerate(slots):
            if slot % 2 != side:
                continue
            product = jnp.dot(rounded_ref[...], k_ref[:, pl.ds(place * rows, rows)], preferred_element_type=F32)
            out_refs[out][...] = product * weights_ref[:, pl.ds(slot * rows, rows)]
            out += 1


def same_kernel(near, far, weights_ref, rounded_ref, near_ref, far_ref, *out_refs):
    contribute(near, far, 0, weights_ref, rounded_ref, near_ref, far_ref, out_refs)


def columns_of(nrhs, *pairs):
    at = lax.broadcasted_iota(jnp.int32, (nrhs, 128), 1)
    table = jnp.zeros((nrhs, 128), F32)
    for place, (x, y) in enumerate(pairs):
        table = jnp.where(at == place, jnp.sum(x * y, axis=1, keepdims=True), table)
    return table


def dots_kernel(amp, nugget_ref, side_ref, w_ref, *refs):
    sums, (u_ref, dots_ref) = refs[:-2], refs[-2:]
    nrhs = side_ref.shape[0]
    total = sums[0][...]
    for ref in sums[1:]:
        total += ref[...]
    b, w = side_ref[...], w_ref[...]
    u = nugget_ref[...] * w + amp * total
    u_ref[...] = u
    upper = columns_of(nrhs, (b, b), (w, w), (w, u))
    lower = columns_of(nrhs, (b, w), (b, u))
    table = jnp.concatenate([upper, lower], axis=0).T
    for place in range(3):
        row = table[place : place + 1]
        part = pl.ds(2 * nrhs * place, 2 * nrhs)
        dots_ref[:, :, part] = jnp.broadcast_to(row[None], (dots_ref.shape[0], 1, 2 * nrhs))


def last_kernel(side_ref, w_ref, u_ref, dots_ref, solution_ref, residual_ref):
    nrhs = side_ref.shape[0]
    row = jnp.sum(dots_ref[...], axis=0)
    width = 2 * nrhs
    at = lax.broadcasted_iota(jnp.int32, (8, width), 0)
    table = jnp.zeros((8, width), F32)
    for place in range(3):
        table = jnp.where(at == place, row[:, place * width : (place + 1) * width], table)
    table = jnp.concatenate([table, jnp.zeros((120, width), F32)], axis=0).T
    bb, ww, wu = (table[:nrhs, at : at + 1] for at in range(3))
    bw, bu = (table[nrhs : 2 * nrhs, at : at + 1] for at in range(2))
    b, w, u = side_ref[...], w_ref[...], u_ref[...]
    b_image = bw + THETA * bb
    alpha = bb / b_image
    keep = 1.0 - alpha * THETA
    norm = keep * keep * bb - 2.0 * keep * alpha * bw + alpha * alpha * ww
    c = keep + norm / bb
    curve = c * c * b_image - c * alpha * (bu + ww + THETA * bw) + alpha * alpha * wu
    step = norm / curve
    direction = c * b - alpha * w
    solution_ref[...] = alpha * b + step * direction
    residual_ref[...] = keep * b - alpha * w - step * (c * w + (c * THETA) * b - alpha * u)


def call(kernel, name, shapes, *operands):
    outs = [jax.ShapeDtypeStruct(shape, dtype) for shape, dtype in shapes]
    return pl.pallas_call(
        kernel,
        out_shape=outs,
        in_specs=[VMEM] * len(operands),
        out_specs=[VMEM] * len(outs),
        compiler_params=PARAMS,
        name=name,
    )(*operands)


def on_device(points, right_side, nugget, scales, pairs):
    nblk = lax.axis_size("blk")
    ngrp = lax.axis_size("grp")
    feat, rows = points.shape
    nrhs = right_side.shape[0]
    total = rows * ngrp
    height = feat + nrhs
    amp = 1.0 / (total + 16) / REACH**4
    plane = Plane(nblk, pairs.shape[1])
    nugget, scales, pairs = nugget[None, :], scales[None, :], pairs.T

    def swap(value, axis, route):
        return lax.ppermute(value, axis, route)

    def from_core(value):
        return swap(value, "blk", [(i ^ 1, i) for i in range(nblk)])

    def from_chip(value, hop):
        return swap(value, "blk", [(plane.there(i, hop), i) for i in range(nblk)])

    def to_chip(value, hop):
        return swap(value, "blk", [(i, plane.there(i, hop)) for i in range(nblk)])

    def across(value, step):
        return swap(value, "grp", [(i ^ step, i) for i in range(ngrp)])

    row_near = points
    step = 1
    while 2 * step < ngrp:
        row_near = jnp.concatenate([row_near, across(row_near, step)], axis=0)
        step *= 2
    row_far = across(row_near, step)
    stacked = jnp.concatenate([points, right_side.astype(BF16)], axis=0)
    stacked = jnp.concatenate([stacked, from_core(stacked)], axis=0)
    if plane.doubling:
        hop = 1
        while 2 * hop < plane.chips:
            stacked = jnp.concatenate([stacked, from_chip(stacked, hop)], axis=0)
            hop *= 2
        others = [from_chip(stacked, hop)]
    else:
        others = [from_chip(stacked, hop) for hop in plane.hops[1:]]
    near = list(range(stacked.shape[0] // height))
    at_slot = {slot: slot - len(near) for slot in range(len(near), plane.slots)}
    far = [slot for slot in at_slot if slot in plane.live]
    row_f, weights, k_near, acc = call(
        functools.partial(near_kernel, plane, near),
        "near",
        [
            ((total, 64), BF16),
            ((1, plane.slots * rows), F32),
            ((total, len(near) * rows), BF16),
            ((nrhs, total), F32),
        ],
        pairs, scales, row_near, row_far, stacked,
    )
    k_far, own, *messages = call(
        functools.partial(far_kernel, far, at_slot, amp),
        "far",
        [((total, len(far) * rows), BF16), ((nrhs, total), F32)] + [((nrhs, total + rows), BF16)] * (ngrp - 1),
        scales, nugget, right_side, row_f, weights, acc, *others,
    )

    messages = [across(message, step) for step, message in enumerate(messages, 1)]
    piece = ((nrhs, rows), F32)
    w, rounded, *cross = call(
        functools.partial(cross_kernel, near, far),
        "cross",
        [piece, ((nrhs, total), BF16)] + [piece] * count_cross(near, far),
        weights, own, k_near, k_far, *messages,
    )
    cross = from_core(jnp.concatenate(cross, axis=0))
    same = call(
        functools.partial(same_kernel, near, far),
        "same",
        [piece] * (len(near) + len(far) - count_cross(near, far)),
        weights, rounded, k_near, k_far,
    )
    pieces = [None] * len(plane.hops)
    for slot, part in zip([slot for slot in near + far if slot % 2 == 0], same):
        pieces[slot // 2] = part
    for at, slot in enumerate([slot for slot in near + far if slot % 2]):
        part = cross[at * nrhs : (at + 1) * nrhs]
        pieces[slot // 2] = part if pieces[slot // 2] is None else pieces[slot // 2] + part
    pieces = [pieces[0]] + [to_chip(part, hop) for part, hop in zip(pieces[1:], plane.hops[1:])]
    u, dots = call(
        functools.partial(dots_kernel, amp),
        "dots",
        [piece, ((nblk * ngrp, 1, 6 * nrhs), F32)],
        nugget, right_side, w, *pieces,
    )
    dots = lax.all_to_all(dots, ("blk", "grp"), 0, 0)
    return call(last_kernel, "outputs", [piece] * 2, right_side, w, u, dots)


def solution(mesh):
    placed = (P(None, ("blk", "grp")), P(None, ("blk", "grp")), P(("blk", "grp")), P(), P())
    return jax.shard_map(
        on_device,
        mesh=mesh,
        in_specs=placed,
        out_specs=(P(None, ("blk", "grp")), P(None, ("blk", "grp"))),
        check_vma=False,
    )
```
